256 devices in a mesh: seq: 64 (over x, y, z_hi, core), section: 4 (over z_lo).
Axes of the slice: x: 4, y: 4, z: 8 (z_hi: 2, z_lo: 4; z = z_hi * 4 + z_lo), core: 2. Of those that a mesh axis runs over, the one named last changes fastest.
Arguments:
- queries: bfloat16 [4, 8192, 2048], P('section', 'seq'), may hold values from -60 to 60
- keys_in: bfloat16 [4, 8192, 2048], P('section', 'seq'), may hold values from -15 to 15
- values: bfloat16 [4, 8192, 2048], P('section', 'seq'), may hold values from -6 to 6
- out_grads: bfloat16 [4, 8192, 2048], P('section', 'seq'), may hold values from -6 to 6
- offsets: int32 [3, 16], replicated, may hold values from 0 to 7
Outputs:
- grad_queries: bfloat16 [4, 8192, 2048], P('section', 'seq')
- grad_keys: bfloat16 [4, 8192, 2048], P('section', 'seq')
- grad_values: bfloat16 [4, 8192, 2048], P('section', 'seq')
The draws below stay inside these ranges and needn't reach their ends.
Inputs may be any that keep to these rules, and one draw needn't show every extreme that they name: Level l uses offsets[l - 1, h] modulo 2^l.
All inputs are finite; a program needn't handle non-finite values.
Results may differ from the reference program's by a relative error of at most 0.029.
Values may be sent and summed in bfloat16 or wider, within the bound.
A program may use at most 64 MiB of HBM per device.

```python
import jax
import jax.numpy as jnp
from jax import lax

TOK_DEV = 128
HEADS = 16
HEAD_DIM = 128
LEVELS = 3
SECTIONS = 4
TOKENS = 8192
WIDTH = 2048
N_SEQ = 64


def pair_draw(key):
    shape = (SECTIONS, TOKENS, HEADS * HEAD_DIM)
    base_keys = jnp.clip(jax.random.normal(jax.random.fold_in(key, 101), shape, jnp.float32), -6.0, 6.0)
    base_queries = jnp.clip(jax.random.normal(jax.random.fold_in(key, 102), shape, jnp.float32), -6.0, 6.0)
    keys_out = base_keys
    queries_out = base_queries
    return (queries_out, keys_out)


def draw_queries(key, part):
    return pair_draw(key)[0].astype(jnp.bfloat16)


def draw_keys_in(key, part):
    return pair_draw(key)[1].astype(jnp.bfloat16)


def plant(result, key, low, high):
    longest = result.shape.index(max(result.shape))
    spots = []
    for shift in (0, 1):
        where = [jax.random.randint(jax.random.fold_in(key, axis), (), 0, length) for axis, length in enumerate(result.shape)]
        where[longest] = (where[longest] + shift) % result.shape[longest]
        spots.append(tuple(where))
    return result.at[spots[0]].set(low).at[spots[1]].set(high)


def block_scale(stream_key, dims, split, low, top_value):
    gain, own = 1.0, jax.random.fold_in(stream_key, 6)
    for dim, parts in split:
        draws = jnp.exp(jax.random.uniform(jax.random.fold_in(own, dim), (parts,), jnp.float32, low / len(split), top_value / len(split)))
        gain = gain * jnp.repeat(draws, dims[dim] // parts).reshape([-1 if axis == dim else 1 for axis in range(len(dims))])
    return gain


def normal_values(own_key, dims, scale, bound, cuts=(), kind=jnp.bfloat16):
    level = block_scale(own_key, dims, cuts, -0.22, 0.18) if cuts else 1.0
    result = jax.random.normal(own_key, dims, jnp.float32) * scale * level
    return jnp.minimum(jnp.maximum(result, -bound), bound).astype(kind)


def setup_inputs(seed: int = 0) -> dict:
    seeds = jax.random.split(jax.random.key(seed), 6)
    return {
        "queries": draw_queries(jax.random.fold_in(seeds[5], 71), 0),
        "keys_in": draw_keys_in(jax.random.fold_in(seeds[5], 71), 0),
        "values": normal_values(seeds[2], (SECTIONS, TOKENS, WIDTH), 1.0, 6.0, ((0, 4), (1, 64))),
        "out_grads": normal_values(seeds[3], (SECTIONS, TOKENS, WIDTH), 1.0, 6.0, ((0, 4), (1, 64))),
        "offsets": plant(jax.random.randint(seeds[4], (LEVELS, HEADS), 0, 2 ** LEVELS), jax.random.fold_in(seeds[4], 1), 0, (2 ** LEVELS) - 1).astype(jnp.int32),
    }


def pick_rows(tile_rows, dilation, chosen):
    row_count, head_count, head_dim = tile_rows.shape
    shaped = tile_rows.reshape(row_count // dilation, dilation, head_count, head_dim)
    keep_mask = jnp.arange(dilation, dtype=jnp.int32)[None, :, None, None] == (chosen % dilation)[None, None, :, None]
    return jnp.sum(jnp.where(keep_mask, shaped, jnp.zeros((), tile_rows.dtype)), axis=1).astype(tile_rows.dtype)


def spread_rows(row_values, dilation, chosen):
    row_count, head_count, head_dim = row_values.shape
    keep_mask = jnp.arange(dilation, dtype=jnp.int32)[None, :, None, None] == (chosen % dilation)[None, None, :, None]
    spread = jnp.where(keep_mask, row_values[:, None], jnp.zeros((), row_values.dtype))
    return spread.reshape(row_count * dilation, head_count, head_dim)


def pick_stat(row_stat, dilation, chosen):
    head_count, row_count = row_stat.shape
    shaped = row_stat.reshape(head_count, row_count // dilation, dilation)
    keep_mask = jnp.arange(dilation, dtype=jnp.int32)[None, None, :] == (chosen % dilation)[:, None, None]
    return jnp.sum(jnp.where(keep_mask, shaped, 0.0), axis=2)


def spread_stat(row_stat, dilation, chosen, fill_value):
    head_count, row_count = row_stat.shape
    keep_mask = jnp.arange(dilation, dtype=jnp.int32)[None, None, :] == (chosen % dilation)[:, None, None]
    return jnp.where(keep_mask, row_stat[:, :, None], fill_value).reshape(head_count, row_count * dilation)


def block_pass(query_rows, key_rows, value_rows, grad_rows, group_keys, group_values, offsets):
    score_scale = HEAD_DIM ** -0.5
    sel_q = [query_rows]
    sel_g = [grad_rows]
    key_sets = [key_rows]
    value_sets = [value_rows]
    for bit_level in range(LEVELS):
        dilation = 2 ** (bit_level + 1)
        chosen = offsets[bit_level]
        sel_q.append(pick_rows(query_rows, dilation, chosen))
        sel_g.append(pick_rows(grad_rows, dilation, chosen))
        key_sets.append(group_keys[bit_level])
        value_sets.append(group_values[bit_level])
    scores = [jnp.einsum("qhe,khe->hqk", sel_q[i].astype(jnp.float32), key_sets[i].astype(jnp.float32)) * score_scale for i in range(LEVELS + 1)]
    part_lse = [jax.nn.logsumexp(level_scores, axis=-1) for level_scores in scores]
    total_lse = part_lse[0]
    for bit_level in range(LEVELS):
        total_lse = jnp.logaddexp(total_lse, spread_stat(part_lse[bit_level + 1], 2 ** (bit_level + 1), offsets[bit_level], -jnp.inf))
    row_lse = [total_lse] + [pick_stat(total_lse, 2 ** (b + 1), offsets[b]) for b in range(LEVELS)]
    weights = [jnp.exp(scores[i] - row_lse[i][:, :, None]) for i in range(LEVELS + 1)]
    rounded = [w.astype(jnp.bfloat16) for w in weights]
    output = jnp.einsum("hqk,khe->qhe", rounded[0].astype(jnp.float32), value_sets[0].astype(jnp.float32))
    for bit_level in range(LEVELS):
        level_out = jnp.einsum("hqk,khe->qhe", rounded[bit_level + 1].astype(jnp.float32), value_sets[bit_level + 1].astype(jnp.float32))
        output = output + spread_rows(level_out, 2 ** (bit_level + 1), offsets[bit_level])
    delta_rows = jnp.sum(grad_rows.astype(jnp.float32) * output, axis=2).T
    row_delta = [delta_rows] + [pick_stat(delta_rows, 2 ** (b + 1), offsets[b]) for b in range(LEVELS)]
    grad_q = jnp.zeros(query_rows.shape, jnp.float32)
    grad_k = jnp.zeros(query_rows.shape, jnp.float32)
    grad_v = jnp.zeros(query_rows.shape, jnp.float32)
    level_keys = []
    level_values = []
    for level_index in range(LEVELS + 1):
        pgrad = jnp.einsum("qhe,khe->hqk", sel_g[level_index].astype(jnp.float32), value_sets[level_index].astype(jnp.float32))
        dscore = weights[level_index] * (pgrad - row_delta[level_index][:, :, None])
        dround = dscore.astype(jnp.bfloat16).astype(jnp.float32)
        q_part = jnp.einsum("hqk,khe->qhe", dround, key_sets[level_index].astype(jnp.float32)) * score_scale
        key_part = jnp.einsum("hqk,qhe->khe", dround, sel_q[level_index].astype(jnp.float32)) * score_scale
        value_part = jnp.einsum("hqk,qhe->khe", rounded[level_index].astype(jnp.float32), sel_g[level_index].astype(jnp.float32))
        if level_index == 0:
            grad_q = grad_q + q_part
            grad_k = grad_k + key_part
            grad_v = grad_v + value_part
        else:
            grad_q = grad_q + spread_rows(q_part, 2 ** level_index, offsets[level_index - 1])
            level_keys.append(key_part)
            level_values.append(value_part)
    return grad_q, grad_k, grad_v, tuple(level_keys), tuple(level_values)


def reference(queries, keys_in, values, out_grads, offsets):
    tile_shape = (N_SEQ, TOK_DEV, HEADS, HEAD_DIM)
    outs_q = []
    outs_k = []
    outs_v = []
    for section_index in range(SECTIONS):
        query_all = queries[section_index].reshape(tile_shape)
        key_all = keys_in[section_index].reshape(tile_shape)
        value_all = values[section_index].reshape(tile_shape)
        grad_all = out_grads[(section_index + 1) % SECTIONS].reshape(tile_shape)
        group_k = []
        group_v = []
        for bit_level in range(LEVELS):
            dilation = 2 ** (bit_level + 1)
            chosen = offsets[bit_level]
            picker = jax.vmap(lambda tile, dilation=dilation, chosen=chosen: pick_rows(tile, dilation, chosen))
            group_k.append(picker(key_all).reshape(N_SEQ // dilation, TOK_DEV, HEADS, HEAD_DIM))
            group_v.append(picker(value_all).reshape(N_SEQ // dilation, TOK_DEV, HEADS, HEAD_DIM))

        def one_block(block_index, query_all=query_all, key_all=key_all, value_all=value_all, grad_all=grad_all, group_k=group_k, group_v=group_v):
            return block_pass(query_all[block_index], key_all[block_index], value_all[block_index], grad_all[block_index],
                              [group_k[b][block_index // (2 ** (b + 1))] for b in range(LEVELS)],
                              [group_v[b][block_index // (2 ** (b + 1))] for b in range(LEVELS)], offsets)

        grad_q, grad_k, grad_v, level_keys, level_values = lax.map(one_block, jnp.arange(N_SEQ, dtype=jnp.int32))
        for bit_level in range(LEVELS):
            dilation = 2 ** (bit_level + 1)
            chosen = offsets[bit_level]
            placer = jax.vmap(lambda rows, dilation=dilation, chosen=chosen: spread_rows(rows, dilation, chosen))
            summed_k = level_keys[bit_level].reshape(N_SEQ // dilation, dilation, TOK_DEV, HEADS, HEAD_DIM).sum(axis=1)
            summed_v = level_values[bit_level].reshape(N_SEQ // dilation, dilation, TOK_DEV, HEADS, HEAD_DIM).sum(axis=1)
            grad_k = grad_k + placer(summed_k.reshape(N_SEQ, TOK_DEV // dilation, HEADS, HEAD_DIM))
            grad_v = grad_v + placer(summed_v.reshape(N_SEQ, TOK_DEV // dilation, HEADS, HEAD_DIM))
        outs_q.append(grad_q.astype(jnp.bfloat16).reshape(TOKENS, WIDTH))
        outs_k.append(grad_k.astype(jnp.bfloat16).reshape(TOKENS, WIDTH))
        outs_v.append(grad_v.astype(jnp.bfloat16).reshape(TOKENS, WIDTH))
    return jnp.stack(outs_q), jnp.stack(outs_k), jnp.stack(outs_v)
```

```python
import functools

import jax
import jax.numpy as jnp
from jax import lax
from jax.experimental import pallas as pl
from jax.experimental.pallas import tpu as pltpu
from jax.sharding import PartitionSpec as P

MESH = pl.DeviceIdType.MESH
LANES = 128
CHUNKS = 4
UNROLL = 2
MASKED = -1e30
OWN = (128, 240)
OWN23 = (192, 240)
OWN3 = (224, 240)
NEXT = (240, 352)
DIAG = (352, 400)
FAR = (400, 448)
FAR3 = (432, 448)
SIDE = ((448, 464), (464, 480), (480, 496), (496, 512))
LEVEL_RUNS = (
    (0, 128), (1, 64), (2, 32), (3, 16), (1, 64), (2, 32), (3, 16), (2, 32), (3, 16), (2, 32), (3, 16), (3, 64),
)
NT = (((1,), (1,)), ((), ()))
TN = (((0,), (0,)), ((), ()))
NN = (((1,), (0,)), ((), ()))


def flipped(index, bit):
    return index + bit - 2 * bit * ((index // bit) % 2)


def product(left, right, dims):
    return lax.dot_general(left, right, dims, preferred_element_type=jnp.float32)


def select_matrix(chosen):
    parts = []
    for level in (1, 2, 3):
        rate = 2**level
        shape = (LANES // rate, LANES)
        column = lax.broadcasted_iota(jnp.int32, shape, 1)
        row = lax.broadcasted_iota(jnp.int32, shape, 0)
        parts.append(column - rate * row == chosen[level])
    return jnp.concatenate([jnp.where(part, 1.0, 0.0) for part in parts], axis=0).astype(jnp.bfloat16)


def level_bias(chosen):
    lane = lax.broadcasted_iota(jnp.int32, (1, LANES), 1)
    rows = {0: jnp.zeros((1, LANES), jnp.float32)}
    for level in (1, 2, 3):
        kept = jnp.bitwise_and(lane, 2**level - 1) == chosen[level]
        rows[level] = jnp.where(kept, 0.0, MASKED)
    return jnp.concatenate([jnp.broadcast_to(rows[level], (count, LANES)) for level, count in LEVEL_RUNS], axis=0)


def kernel(
    heads, sections, scale, off, q_in, k_in, v_in, g_in, dq_out, dk_out, dv_out,
    kv, qb, gb, grads, own, from_next, from_side, from_far, far_sum, dqb, dkb, dvb,
    load_sem, send_sem, recv_sem, store_sem,
):
    per = heads // CHUNKS
    seq = lax.axis_index("seq")
    section = lax.axis_index("section")
    before = (seq, (section + sections - 1) % sections)
    after = (seq, (section + 1) % sections)
    one = (flipped(seq, 1), section)
    two = (flipped(seq, 2), section)
    four = (flipped(seq, 4), section)
    five = (flipped(flipped(seq, 4), 1), section)

    def load(source, tensor, head):
        columns = pl.ds(pl.multiple_of(head * LANES, LANES), LANES)
        return pltpu.make_async_copy(
            source.at[0, :, columns], kv.at[head, tensor, pl.ds(0, LANES)], load_sem.at[tensor, head]
        )

    load_q = pltpu.make_async_copy(q_in.at[0], qb, load_sem.at[2, 0])
    for head in range(heads):
        load(k_in, 0, head).start()
        load(v_in, 1, head).start()
    load_q.start()
    barrier = pltpu.get_barrier_semaphore()
    for device in (before, after, one, two, four, five):
        pl.semaphore_signal(barrier, inc=1, device_id=device, device_id_type=MESH)

    def remote(kind, chunk, source, target, device):
        return pltpu.make_async_remote_copy(
            src_ref=source, dst_ref=target, send_sem=send_sem.at[kind, chunk], recv_sem=recv_sem.at[kind, chunk],
            device_id=device, device_id_type=MESH,
        )

    def key_copy(kind, chunk, source, target, device):
        some = pl.ds(chunk * per, per)
        return remote(
            kind, chunk, kv.at[some, :, pl.ds(source[0], source[1] - source[0])],
            kv.at[some, :, pl.ds(target[0], target[1] - target[0])], device,
        )

    def copies(chunk):
        some = pl.ds(chunk * per, per)
        columns = pl.ds(chunk * per * LANES, per * LANES)
        return {
            "far": key_copy(0, chunk, OWN23, FAR, two),
            "grad": remote(1, chunk, g_in.at[0, :, columns], gb.at[:, columns], before),
            "next": key_copy(2, chunk, OWN, NEXT, one),
            "side0": key_copy(3, chunk, OWN3, SIDE[0], four),
            "side1": key_copy(4, chunk, OWN3, SIDE[1], five),
            "diag": key_copy(5, chunk, FAR, DIAG, one),
            "side2": key_copy(6, chunk, FAR3, SIDE[2], four),
            "side3": key_copy(7, chunk, FAR3, SIDE[3], five),
            "back_next": remote(8, chunk, grads.at[some, :, pl.ds(0, 160)], from_next.at[some], one),
            "back0": remote(9, chunk, grads.at[some, :, pl.ds(208, 16)], from_side.at[0, some], four),
            "back1": remote(10, chunk, grads.at[some, :, pl.ds(224, 16)], from_side.at[1, some], five),
            "back2": remote(11, chunk, grads.at[some, :, pl.ds(240, 16)], from_side.at[2, some], four),
            "back3": remote(12, chunk, grads.at[some, :, pl.ds(256, 16)], from_side.at[3, some], five),
            "back_far": remote(13, chunk, far_sum.at[some], from_far.at[some], two),
        }

    moves = [copies(chunk) for chunk in range(CHUNKS)]

    def head_offsets(head):
        return [None] + [jnp.bitwise_and(off[level - 1, head], 2**level - 1) for level in (1, 2, 3)]

    def select(chunk):
        def one_head(head, carry):
            load(k_in, 0, head).wait()
            load(v_in, 1, head).wait()
            picker = select_matrix(head_offsets(head))
            for tensor in range(2):
                kept = product(picker, kv[head, tensor, pl.ds(0, LANES)], NN)
                kv[head, tensor, pl.ds(OWN[0], 112)] = kept.astype(jnp.bfloat16)
            return carry

        lax.fori_loop(chunk * per, (chunk + 1) * per, one_head, 0)

    def attend(head):
        columns = pl.ds(pl.multiple_of(head * LANES, LANES), LANES)
        query = qb[:, columns]
        grad = gb[:, columns]
        keys = kv[head, 0]
        vals = kv[head, 1]
        scores = product(keys, query, NT) * scale + level_bias(head_offsets(head))
        top = jnp.max(scores, axis=0, keepdims=True)
        raised = jnp.exp(scores - top)
        weights = raised * (1.0 / jnp.sum(raised, axis=0, keepdims=True))
        rounded = weights.astype(jnp.bfloat16)
        pgrad = product(vals, grad, NT)
        delta = jnp.sum(rounded.astype(jnp.float32) * pgrad, axis=0, keepdims=True)
        dround = (weights * (pgrad - delta)).astype(jnp.bfloat16)
        dqb[:, columns] = (product(dround, keys, TN) * scale).astype(jnp.bfloat16)
        key_grad = product(dround, query, NN) * scale
        value_grad = product(rounded, grad, NN)
        own[head, 0] = key_grad[:240]
        own[head, 1] = value_grad[:240]
        grads[head, 0] = key_grad[240:].astype(jnp.bfloat16)
        grads[head, 1] = value_grad[240:].astype(jnp.bfloat16)

    def compute(chunk):
        def some_heads(step, carry):
            for lane in range(UNROLL):
                attend(chunk * per + step * UNROLL + lane)
            return carry

        lax.fori_loop(0, per // UNROLL, some_heads, 0)

    def reduce(chunk):
        def one_head(head, carry):
            for tensor in range(2):
                total = grads[head, tensor, pl.ds(160, 48)].astype(jnp.float32)
                total = total + from_next[head, tensor, pl.ds(112, 48)].astype(jnp.float32)
                last = from_side[2, head, tensor].astype(jnp.float32) + from_side[3, head, tensor].astype(jnp.float32)
                far_sum[head, tensor, pl.ds(0, 32)] = total[:32].astype(jnp.bfloat16)
                far_sum[head, tensor, pl.ds(32, 16)] = (total[32:] + last).astype(jnp.bfloat16)
            return carry

        for name in ("back_next", "back0", "back1", "back2", "back3"):
            moves[chunk][name].wait_recv()
        lax.fori_loop(chunk * per, (chunk + 1) * per, one_head, 0)
        moves[chunk]["back_far"].start()

    def store(chunk, buffer, output, index):
        columns = pl.ds(chunk * per * LANES, per * LANES)
        return pltpu.make_async_copy(buffer.at[:, columns], output.at[0, :, columns], store_sem.at[index, chunk])

    def finish(chunk):
        def one_head(head, carry):
            columns = pl.ds(pl.multiple_of(head * LANES, LANES), LANES)
            picker = select_matrix(head_offsets(head))
            for tensor, buffer in ((0, dkb), (1, dvb)):
                near = own[head, tensor, pl.ds(128, 112)] + from_next[head, tensor, pl.ds(0, 112)].astype(jnp.float32)
                far = from_far[head, tensor].astype(jnp.float32)
                side = from_side[0, head, tensor].astype(jnp.float32) + from_side[1, head, tensor].astype(jnp.float32)
                rows = jnp.concatenate([near[:64], near[64:96] + far[:32], near[96:] + far[32:] + side], axis=0)
                spread = product(picker, rows.astype(jnp.bfloat16), TN)
                buffer[:, columns] = (own[head, tensor, pl.ds(0, 128)] + spread).astype(jnp.bfloat16)
            return carry

        moves[chunk]["back_far"].wait_recv()
        lax.fori_loop(chunk * per, (chunk + 1) * per, one_head, 0)
        store(chunk, dkb, dk_out, 1).start()
        store(chunk, dvb, dv_out, 2).start()

    for chunk in range(CHUNKS):
        select(chunk)
        if chunk == 0:
            pl.semaphore_wait(barrier, 6)
        for name in ("far", "grad", "next", "side0", "side1"):
            moves[chunk][name].start()
    load_q.wait()
    for chunk in range(CHUNKS):
        moves[chunk]["far"].wait_recv()
        for name in ("diag", "side2", "side3"):
            moves[chunk][name].start()
        if chunk > 0:
            reduce(chunk - 1)
        for name in ("next", "side0", "side1", "grad", "diag", "side2", "side3"):
            moves[chunk][name].wait_recv()
        compute(chunk)
        for name in ("back_next", "back2", "back3", "back0", "back1"):
            moves[chunk][name].start()
        store(chunk, dqb, dq_out, 0).start()
    reduce(CHUNKS - 1)
    for chunk in range(CHUNKS):
        finish(chunk)
    for chunk in range(CHUNKS):
        for move in moves[chunk].values():
            move.wait_send()
        store(chunk, dqb, dq_out, 0).wait()
        store(chunk, dkb, dk_out, 1).wait()
        store(chunk, dvb, dv_out, 2).wait()


def solution(mesh):
    sections = mesh.shape["section"]

    def per_device(queries, keys_in, values, out_grads, offsets):
        heads = offsets.shape[1]
        rows = queries.shape[1]
        width = queries.shape[2]
        scale = (width // heads) ** (-0.5)
        shape = jax.ShapeDtypeStruct((1, rows, width), jnp.bfloat16)
        kinds = 14
        return pl.pallas_call(
            functools.partial(kernel, heads, sections, scale),
            out_shape=(shape, shape, shape),
            in_specs=[pl.BlockSpec(memory_space=pltpu.SMEM)] + [pl.BlockSpec(memory_space=pl.ANY)] * 4,
            out_specs=(pl.BlockSpec(memory_space=pl.ANY),) * 3,
            scratch_shapes=[
                pltpu.VMEM((heads, 2, 512, LANES), jnp.bfloat16),
                pltpu.VMEM((rows, width), jnp.bfloat16),
                pltpu.VMEM((rows, width), jnp.bfloat16),
                pltpu.VMEM((heads, 2, 272, LANES), jnp.bfloat16),
                pltpu.VMEM((heads, 2, 240, LANES), jnp.float32),
                pltpu.VMEM((heads, 2, 160, LANES), jnp.bfloat16),
                pltpu.VMEM((4, heads, 2, 16, LANES), jnp.bfloat16),
                pltpu.VMEM((heads, 2, 48, LANES), jnp.bfloat16),
                pltpu.VMEM((heads, 2, 48, LANES), jnp.bfloat16),
                pltpu.VMEM((rows, width), jnp.bfloat16),
                pltpu.VMEM((rows, width), jnp.bfloat16),
                pltpu.VMEM((rows, width), jnp.bfloat16),
                pltpu.SemaphoreType.DMA((3, heads)),
                pltpu.SemaphoreType.DMA((kinds, CHUNKS)),
                pltpu.SemaphoreType.DMA((kinds, CHUNKS)),
                pltpu.SemaphoreType.DMA((3, CHUNKS)),
            ],
            compiler_params=pltpu.CompilerParams(
                collective_id=0, has_side_effects=True, vmem_limit_bytes=48 * 2**20
            ),
        )(offsets, queries, keys_in, values, out_grads)

    spec = P("section", "seq", None)
    return jax.shard_map(
        per_device, mesh=mesh, in_specs=(spec, spec, spec, spec, P()), out_specs=(spec, spec, spec), check_vma=False
    )
```

```python
import functools

import jax
import jax.numpy as jnp
from jax import lax
from jax.experimental import pallas as pl
from jax.experimental.pallas import tpu as pltpu
from jax.sharding import PartitionSpec as P

MESH = pl.DeviceIdType.MESH
LANES = 128
CHUNKS = 4
UNROLL = 2
FAR_GROUP = 4
PLAN = "b0 g0 g1 g2 g3 s0 x0 s1 x1 s2 s3 n0 x2 n1 x3 n2 n3 f0 f1 a0 f2 a1 f3 a2 z0 a3 z1 z2 z3"
MASKED = -1e30
LEVEL_RUNS = ((0, 128), (1, 64), (2, 32), (3, 16), (3, 32), (2, 32), (3, 16), (1, 64))
KEYS = 384
CROSS = (192, 128)
NT = (((1,), (1,)), ((), ()))
TN = (((0,), (0,)), ((), ()))
NN = (((1,), (0,)), ((), ()))


def flipped(index, bit):
    return index + bit - 2 * bit * ((index // bit) % 2)


def product(left, right, dims):
    return lax.dot_general(left, right, dims, preferred_element_type=jnp.float32)


def select_matrix(chosen, levels):
    parts = []
    for level in levels:
        rate = 2**level
        shape = (LANES // rate, LANES)
        column = lax.broadcasted_iota(jnp.int32, shape, 1)
        row = lax.broadcasted_iota(jnp.int32, shape, 0)
        parts.append(jnp.where(column - rate * row == chosen[level], 1.0, 0.0))
    return jnp.concatenate(parts, axis=0).astype(jnp.bfloat16)


def level_rows(chosen):
    lane = lax.broadcasted_iota(jnp.int32, (1, LANES), 1)
    rows = {0: jnp.zeros((1, LANES), jnp.float32)}
    for level in (1, 2, 3):
        rows[level] = jnp.where(jnp.bitwise_and(lane, 2**level - 1) == chosen[level], 0.0, MASKED)
    return rows


def exact_parts(rows):
    high = rows.astype(jnp.bfloat16).astype(jnp.float32)
    rest = rows - high
    middle = rest.astype(jnp.bfloat16).astype(jnp.float32)
    return [high, middle, rest - middle]


def stacked_parts(rows):
    parts = exact_parts(rows)
    blank = jnp.zeros((16 - 9, rows.shape[1]), jnp.float32)
    return jnp.concatenate(parts + [blank], axis=0)


def joined_parts(moved, base):
    rows = moved[base : base + 3] + moved[base + 3 : base + 6] + moved[base + 6 : base + 9]
    return rows[0:1], rows[1:2], rows[2:3]


def kernel(
    heads, sections, scale, off, q_in, k_in, v_in, g_in, dq_out, dk_out, dv_out,
    kv, qb, gb, gl, q_send, g_send, q_far, g_far, raised_buf, pgrad_buf, near_stat, far_stat, total_send, total,
    cross, dq_send, dq_far, dq_near, own, grads, from_next, from_side, dqb, dkb, dvb,
    load_sem, send_sem, recv_sem, store_sem,
):
    per = heads // CHUNKS
    seq = lax.axis_index("seq")
    section = lax.axis_index("section")
    prior = (section + sections - 1) % sections
    later = (section + 1) % sections
    before = (seq, prior)
    after = (seq, later)
    one = (flipped(seq, 1), section)
    two = (flipped(seq, 2), section)
    four = (flipped(seq, 4), section)
    five = (flipped(flipped(seq, 4), 1), section)
    two_before = (flipped(seq, 2), prior)
    two_after = (flipped(seq, 2), later)

    def lanes_of(head):
        return pl.ds(pl.multiple_of(head * LANES, LANES), LANES)

    def load(source, tensor, head):
        return pltpu.make_async_copy(
            source.at[0, :, lanes_of(head)], kv.at[head, tensor, pl.ds(0, LANES)], load_sem.at[tensor, head]
        )

    load_q = pltpu.make_async_copy(q_in.at[0], qb, load_sem.at[2, 0])
    load_g = pltpu.make_async_copy(g_in.at[0], gl, load_sem.at[3, 0])
    barrier = pltpu.get_barrier_semaphore()
    friends = (before, after, one, two, four, five, two_before, two_after)
    for device in friends:
        pl.semaphore_signal(barrier, inc=1, device_id=device, device_id_type=MESH)
    load_q.start()
    load_g.start()
    for head in range(heads):
        load(k_in, 0, head).start()
        load(v_in, 1, head).start()

    def copies(chunk):
        some = pl.ds(chunk * per, per)
        columns = pl.ds(chunk * per * LANES, per * LANES)

        def remote(kind, source, target, device):
            return pltpu.make_async_remote_copy(
                src_ref=source, dst_ref=target, send_sem=send_sem.at[kind, chunk],
                recv_sem=recv_sem.at[kind, chunk], device_id=device, device_id_type=MESH,
            )

        def keys(start, size):
            return kv.at[some, :, pl.ds(start, size)]

        return {
            "grad": remote(0, gl.at[:, columns], gb.at[:, columns], before),
            "grad_far": remote(1, g_send.at[some], g_far.at[some], two_before),
            "query_far": remote(2, q_send.at[some], q_far.at[some], two),
            "next1": remote(3, keys(128, 64), keys(320, 64), one),
            "next23": remote(4, keys(192, 48), keys(272, 48), one),
            "side4": remote(5, keys(224, 16), keys(240, 16), four),
            "side5": remote(6, keys(224, 16), keys(256, 16), five),
            "stat": remote(7, near_stat.at[some], far_stat.at[some], two),
            "total": remote(8, total_send.at[some], total.at[some], two),
            "dq": remote(9, dq_send.at[some], dq_far.at[some], two),
            "back_next": remote(10, grads.at[some, :, pl.ds(32, 112)], from_next.at[some], one),
            "back4": remote(11, grads.at[some, :, pl.ds(0, 16)], from_side.at[0, some], four),
            "back5": remote(12, grads.at[some, :, pl.ds(16, 16)], from_side.at[1, some], five),
        }

    moves = [copies(chunk) for chunk in range(CHUNKS)]

    def start(chunk, *names):
        for name in names:
            moves[chunk][name].start()

    def arrived(chunk, *names):
        for name in names:
            moves[chunk][name].wait_recv()

    def offsets(head):
        return [None] + [jnp.bitwise_and(off[level - 1, head], 2**level - 1) for level in (1, 2, 3)]

    def for_groups(chunk, body, size):
        def some_heads(step, carry):
            body([chunk * per + step * size + lane for lane in range(size)])
            return carry

        lax.fori_loop(0, per // size, some_heads, 0)

    def for_heads(chunk, body, unroll):
        def some_heads(step, carry):
            for lane in range(unroll):
                body(chunk * per + step * unroll + lane)
            return carry

        lax.fori_loop(0, per // unroll, some_heads, 0)

    def select(head):
        load(k_in, 0, head).wait()
        load(v_in, 1, head).wait()
        picker = select_matrix(offsets(head), (1, 2, 3))
        for tensor in range(2):
            kept = product(picker, kv[head, tensor, pl.ds(0, LANES)], NN)
            kv[head, tensor, pl.ds(128, 112)] = kept.astype(jnp.bfloat16)
        q_send[head] = product(picker[64:], qb[:, lanes_of(head)], NN).astype(jnp.bfloat16)
        g_send[head] = product(picker[64:], gl[:, lanes_of(head)], NN).astype(jnp.bfloat16)

    def near(head):
        query = qb[:, lanes_of(head)]
        grad = gb[:, lanes_of(head)]
        rows = level_rows(offsets(head))
        bias = jnp.concatenate([jnp.broadcast_to(rows[level], (count, LANES)) for level, count in LEVEL_RUNS], axis=0)
        scores = product(kv[head, 0], query, NT) * scale + bias
        top = jnp.max(scores, axis=0, keepdims=True)
        raised = jnp.exp(scores - top)
        pgrad = product(kv[head, 1], grad, NT)
        raised_buf[head] = raised
        pgrad_buf[head] = pgrad
        norm = jnp.sum(raised, axis=0, keepdims=True)
        moment = jnp.sum(raised * pgrad, axis=0, keepdims=True)
        near_stat[head] = jnp.concatenate([top, norm, moment, jnp.zeros((5, LANES), jnp.float32)], axis=0)

    def far(group):
        chosen = [offsets(head) for head in group]
        pickers = [select_matrix(item, (2, 3)) for item in chosen]
        rows = [level_rows(item) for item in chosen]
        keys = [kv[head, 0, pl.ds(*CROSS)] for head in group]
        row = lax.broadcasted_iota(jnp.int32, (LANES, 48), 0)
        column = lax.broadcasted_iota(jnp.int32, (LANES, 48), 1)
        second = jnp.logical_or(row < 32, jnp.logical_and(row >= 80, row < 112))
        same = second == (column < 32)
        scores = [product(item, q_far[head], NT) for item, head in zip(keys, group)]
        pgrads = [product(kv[head, 1, pl.ds(*CROSS)], g_far[head], NT) for head in group]
        scores = [jnp.where(same, item * scale, MASKED) for item in scores]
        tops = [jnp.max(item, axis=0, keepdims=True) for item in scores]
        raised = [jnp.exp(item - top) for item, top in zip(scores, tops)]
        norms = [jnp.sum(item, axis=0, keepdims=True) for item in raised]
        moments = [jnp.sum(item * pgrad, axis=0, keepdims=True) for item, pgrad in zip(raised, pgrads)]
        spreads = []
        for index in range(len(group)):
            parts = stacked_parts(jnp.concatenate([tops[index], norms[index], moments[index]], axis=0))
            is_second = lax.broadcasted_iota(jnp.int32, parts.shape, 1) < 32
            both = jnp.concatenate([jnp.where(is_second, parts, 0.0), jnp.where(is_second, 0.0, parts)], axis=0)
            spreads.append(product(both.astype(jnp.bfloat16), pickers[index], NN))
        picked = []
        for index, head in enumerate(group):
            sets = [(far_stat[head, pl.ds(0, 1)], far_stat[head, pl.ds(1, 1)], far_stat[head, pl.ds(2, 1)])]
            for level, base in ((2, 0), (3, 16)):
                level_top, level_norm, level_moment = joined_parts(spreads[index], base)
                sets.append((level_top + rows[index][level], level_norm, level_moment))
            highest = functools.reduce(jnp.maximum, [item[0] for item in sets])
            shares = [jnp.exp(item[0] - highest) for item in sets]
            inverse = 1.0 / sum(share * item[1] for share, item in zip(shares, sets))
            delta = inverse * sum(share * item[2] for share, item in zip(shares, sets))
            total_rows = jnp.concatenate([highest, inverse, delta], axis=0)
            total_send[head] = jnp.concatenate([total_rows, jnp.zeros((5, LANES), jnp.float32)], axis=0)
            picked.append(product(stacked_parts(total_rows).astype(jnp.bfloat16), pickers[index], NT))
        rounded, drounds = [], []
        for index in range(len(group)):
            far_top, far_inverse, far_delta = joined_parts(picked[index], 0)
            weights = raised[index] * (jnp.exp(tops[index] - far_top) * far_inverse)
            rounded.append(weights.astype(jnp.bfloat16))
            drounds.append((weights * (pgrads[index] - far_delta)).astype(jnp.bfloat16))
        for index, head in enumerate(group):
            dq_send[head] = (product(drounds[index], keys[index], TN) * scale).astype(jnp.bfloat16)
            cross[head, 0] = product(drounds[index], q_far[head], NN) * scale
            cross[head, 1] = product(rounded[index], g_far[head], NN)

    def attend(head):
        query = qb[:, lanes_of(head)]
        grad = gb[:, lanes_of(head)]
        share = jnp.exp(near_stat[head, pl.ds(0, 1)] - total[head, pl.ds(0, 1)]) * total[head, pl.ds(1, 1)]
        weights = raised_buf[head] * share
        rounded = weights.astype(jnp.bfloat16)
        dround = (weights * (pgrad_buf[head] - total[head, pl.ds(2, 1)])).astype(jnp.bfloat16)
        dq_near[:, lanes_of(head)] = product(dround, kv[head, 0], TN) * scale
        sums = (product(dround, query, NN) * scale, product(rounded, grad, NN))
        for tensor in range(2):
            middle = sums[tensor][192:320] + cross[head, tensor]
            own[head, tensor, pl.ds(0, 192)] = sums[tensor][:192]
            own[head, tensor, pl.ds(192, 48)] = middle[:48]
            grads[head, tensor, pl.ds(0, 80)] = middle[48:].astype(jnp.bfloat16)
            grads[head, tensor, pl.ds(80, 64)] = sums[tensor][320:].astype(jnp.bfloat16)

    def finish(head):
        columns = lanes_of(head)
        picker = select_matrix(offsets(head), (1, 2, 3))
        for tensor, buffer in ((0, dkb), (1, dvb)):
            mine = own[head, tensor, pl.ds(128, 112)]
            sent = from_next[head, tensor].astype(jnp.float32)
            side = from_side[0, head, tensor].astype(jnp.float32) + from_side[1, head, tensor].astype(jnp.float32)
            rows = jnp.concatenate(
                [mine[:64] + sent[48:], mine[64:96] + sent[:32], mine[96:] + sent[32:48] + side], axis=0
            )
            spread = product(picker, rows.astype(jnp.bfloat16), TN)
            buffer[:, columns] = (own[head, tensor, pl.ds(0, 128)] + spread).astype(jnp.bfloat16)
        spread = product(picker[64:], dq_far[head], TN)
        dqb[:, columns] = (dq_near[:, columns] + spread).astype(jnp.bfloat16)

    def store(chunk, buffer, output, index):
        columns = pl.ds(chunk * per * LANES, per * LANES)
        return pltpu.make_async_copy(buffer.at[:, columns], output.at[0, :, columns], store_sem.at[index, chunk])

    outputs = ((dqb, dq_out, 0), (dkb, dk_out, 1), (dvb, dv_out, 2))

    load_q.wait()
    load_g.wait()

    def select_step(chunk):
        for_heads(chunk, select, UNROLL)
        start(chunk, "next1", "next23", "side4", "side5")

    def send_step(chunk):
        start(chunk, "grad_far", "query_far")

    def near_step(chunk):
        arrived(chunk, "next1", "next23", "side4", "side5", "grad")
        for_heads(chunk, near, UNROLL)
        start(chunk, "stat")

    def far_step(chunk):
        arrived(chunk, "query_far", "grad_far", "stat")
        for_groups(chunk, far, min(FAR_GROUP, per))
        start(chunk, "total", "dq")

    def attend_step(chunk):
        arrived(chunk, "total")
        for_heads(chunk, attend, UNROLL)
        start(chunk, "back_next", "back4", "back5")

    def finish_step(chunk):
        arrived(chunk, "back_next", "back4", "back5", "dq")
        for_heads(chunk, finish, UNROLL)
        for item in outputs:
            store(chunk, *item).start()

    steps = {
        "b": lambda chunk: pl.semaphore_wait(barrier, len(friends)), "g": lambda chunk: start(chunk, "grad"),
        "s": select_step, "x": send_step, "n": near_step, "f": far_step, "a": attend_step, "z": finish_step,
    }
    for step in PLAN.split():
        steps[step[0]](int(step[1:]))
    for chunk in range(CHUNKS):
        for move in moves[chunk].values():
            move.wait_send()
        for item in outputs:
            store(chunk, *item).wait()


def write_out(*refs):
    copies = [pltpu.make_async_copy(refs[index], refs[index + 3], refs[6].at[index]) for index in range(3)]
    for copy in copies:
        copy.start()
    for copy in copies:
        copy.wait()


def solution(mesh):
    sections = mesh.shape["section"]

    def per_device(queries, keys_in, values, out_grads, offsets):
        heads = offsets.shape[1]
        rows = queries.shape[1]
        width = queries.shape[2]
        scale = (width // heads) ** (-0.5)
        shape = jax.ShapeDtypeStruct((1, rows, width), jnp.bfloat16)
        kinds = 13
        narrow = jnp.bfloat16
        wide = jnp.float32
        results = pl.pallas_call(
            functools.partial(kernel, heads, sections, scale),
            out_shape=(pltpu.VMEM(shape.shape, shape.dtype),) * 3,
            in_specs=[pl.BlockSpec(memory_space=pltpu.SMEM)] + [pl.BlockSpec(memory_space=pltpu.HBM)] * 4,
            out_specs=(pl.BlockSpec(memory_space=pltpu.VMEM),) * 3,
            scratch_shapes=[
                pltpu.VMEM((heads, 2, KEYS, LANES), narrow),
                pltpu.VMEM((rows, width), narrow),
                pltpu.VMEM((rows, width), narrow),
                pltpu.VMEM((rows, width), narrow),
                pltpu.VMEM((heads, 48, LANES), narrow),
                pltpu.VMEM((heads, 48, LANES), narrow),
                pltpu.VMEM((heads, 48, LANES), narrow),
                pltpu.VMEM((heads, 48, LANES), narrow),
                pltpu.VMEM((heads, KEYS, LANES), wide),
                pltpu.VMEM((heads, KEYS, LANES), wide),
                pltpu.VMEM((heads, 8, LANES), wide),
                pltpu.VMEM((heads, 8, LANES), wide),
                pltpu.VMEM((heads, 8, LANES), wide),
                pltpu.VMEM((heads, 8, LANES), wide),
                pltpu.VMEM((heads, 2, LANES, LANES), wide),
                pltpu.VMEM((heads, 48, LANES), narrow),
                pltpu.VMEM((heads, 48, LANES), narrow),
                pltpu.VMEM((rows, width), wide),
                pltpu.VMEM((heads, 2, 240, LANES), wide),
                pltpu.VMEM((heads, 2, 144, LANES), narrow),
                pltpu.VMEM((heads, 2, 112, LANES), narrow),
                pltpu.VMEM((2, heads, 2, 16, LANES), narrow),
                pltpu.VMEM((rows, width), narrow),
                pltpu.VMEM((rows, width), narrow),
                pltpu.VMEM((rows, width), narrow),
                pltpu.SemaphoreType.DMA((4, heads)),
                pltpu.SemaphoreType.DMA((kinds, CHUNKS)),
                pltpu.SemaphoreType.DMA((kinds, CHUNKS)),
                pltpu.SemaphoreType.DMA((3, CHUNKS)),
            ],
            compiler_params=pltpu.CompilerParams(
                collective_id=0, has_side_effects=True, vmem_limit_bytes=58 * 2**20
            ),
        )(offsets, queries, keys_in, values, out_grads)
        return pl.pallas_call(
            write_out,
            out_shape=(shape, shape, shape),
            in_specs=[pl.BlockSpec(memory_space=pltpu.VMEM)] * 3,
            out_specs=(pl.BlockSpec(memory_space=pltpu.HBM),) * 3,
            scratch_shapes=[pltpu.SemaphoreType.DMA((3,))],
            compiler_params=pltpu.CompilerParams(vmem_limit_bytes=2**20),
        )(*results)

    spec = P("section", "seq", None)
    return jax.shard_map(
        per_device, mesh=mesh, in_specs=(spec, spec, spec, spec, P()), out_specs=(spec, spec, spec), check_vma=False
    )
```
